128 devices in a mesh: llm: 4 (over x), enc: 32 (over y, z, core).
Axes of the slice: x: 4, y: 4, z: 4, core: 2. Of those that a mesh axis runs over, the one named last changes fastest.
Arguments:
- token_gradient: bfloat16 [256, 128, 8192], P('enc', None, 'llm'), may hold values from -6 to 6
- projection: bfloat16 [1280, 8192], P(None, 'llm'), may hold values from -0.0625 to 0.0625
- clip_length: int32 [512], P('enc'), may hold values from 16 to 32, as said below
- clip_offset: int32 [512], P('enc'), may hold values from 0 to 96, as said below
- clip_home: int32 [512], P('enc'), may hold values from 0 to 511, as said below
- block_input: bfloat16 [512, 32, 1280], P('enc'), may hold values from -6 to 6
- block_output: bfloat16 [512, 32, 1280], P('enc'), may hold values from -6 to 6
- norm_gain: float32 [1280], replicated, may hold values from 0.1 to 1.9
- norm_bias: float32 [1280], replicated, may hold values from -3 to 3
- up_weight: bfloat16 [1280, 5120], P('enc', 'llm'), may hold values from -0.15625 to 0.15625
- up_bias: float32 [5120], P('llm'), may hold values from -3 to 3
- down_weight: bfloat16 [5120, 1280], P('llm', 'enc'), may hold values from -0.078125 to 0.078125
- post_gain: float32 [1280], replicated, may hold values from 0.1 to 1.9
Outputs:
- input_gradient: bfloat16 [512, 32, 1280], P('enc', None, 'llm')
- up_gradient: float32 [1280, 5120], P('enc', 'llm')
- down_gradient: float32 [5120, 1280], P('llm', 'enc')
The draws below stay inside these ranges and needn't reach their ends.
Inputs may be any that keep to these rules, and one draw needn't show every extreme that they name: `clip_length`: each entry of an aligned block of 16 entries is at most 32, and every block holds one entry equal to 32. Clip k starts in part k % 2 of its sequence, the parts being 64 rows long, and clip_offset + 32 stays within that part. `clip_home`: A permutation of the 512 encoder slots; slot j belongs to encoder index j // 16; the clips of one aligned block of 16 entries go to one encoder index at most 1 times, and some encoder index receives exactly 1 of them.
All inputs are finite; a program needn't handle non-finite values.
Results may differ from the reference program's by a relative error of at most 0.0068.
Values may be sent and summed in bfloat16 or wider, within the bound.
No kernel may reach another device: no remote copies, remote signals or barrier semaphores. Data moves between devices by JAX's collectives and lax.ppermute only.
A program may use at most 128 MiB of HBM per device.

```python
import jax
import jax.numpy as jnp
from jax import lax

D = 1280
FF = 5120
HL = 8192
CLIPS_DEV = 16
FRAMES = 32
CPS = 2
SEQ_LEN = 128
CLIPS = 512
SEQS = 256
N_ENC = 32


def draw_clip_home(key, part):
    base_key = jax.random.fold_in(key, 101)
    sender_order = jax.random.permutation(jax.random.fold_in(base_key, 1), N_ENC)
    target_order = jax.random.permutation(jax.random.fold_in(base_key, 2), N_ENC)
    slot_key = jax.random.fold_in(base_key, 3)
    clip_index = jnp.arange(CLIPS, dtype=jnp.int32)
    sender = clip_index // CLIPS_DEV
    within = clip_index % CLIPS_DEV
    target = target_order[(sender_order[sender] + within) % N_ENC]

    def slot_order(receiver):
        return jax.random.permutation(jax.random.fold_in(slot_key, receiver), CLIPS_DEV)
    slot_tables = jax.vmap(slot_order)(jnp.arange(N_ENC, dtype=jnp.int32))
    chosen_slot = slot_tables[target, within]
    return (target * CLIPS_DEV + chosen_slot).astype(jnp.int32)


def draw_clip_length(key, part):
    base_key = jax.random.fold_in(key, 202)
    lengths = jax.random.randint(jax.random.fold_in(base_key, 1), (CLIPS,), FRAMES // 2, FRAMES + 1)
    longest = jax.random.randint(jax.random.fold_in(base_key, 2), (N_ENC,), 0, CLIPS_DEV)
    clip_index = jnp.arange(CLIPS, dtype=jnp.int32)
    full_clip = clip_index % CLIPS_DEV == longest[clip_index // CLIPS_DEV]
    return jnp.where(full_clip, FRAMES, lengths).astype(jnp.int32)


def draw_clip_offset(key, part):
    base_key = jax.random.fold_in(key, 303)
    segment = SEQ_LEN // CPS
    clip_index = jnp.arange(CLIPS, dtype=jnp.int32)
    segment_start = clip_index % CPS * segment
    extra_rows = jax.random.randint(jax.random.fold_in(base_key, 1), (CLIPS,), 0, segment - FRAMES + 1)
    return (segment_start + extra_rows).astype(jnp.int32)


def block_scale(own_key, dims, pieces, least, top_value):
    gain = 1.0
    for dim, parts in pieces:
        heights = jax.random.uniform(jax.random.fold_in(jax.random.fold_in(own_key, 6), dim), (parts,), jnp.float32, least / len(pieces), top_value / len(pieces))
        gain = gain * jnp.repeat(jnp.exp(heights), dims[dim] // parts).reshape((-1,) + (1,) * (len(dims) - 1 - dim))
    return gain


def noise(stream_key, extent, spread, limit, shards=(), kind=jnp.bfloat16):
    loudness = block_scale(stream_key, extent, shards, -0.22, 0.18) if shards else 1.0
    result = jax.random.normal(stream_key, extent, jnp.float32) * spread * loudness
    return jnp.minimum(jnp.maximum(result, -limit), limit).astype(kind)


def setup_inputs(seed: int = 0) -> dict:
    seeds = jax.random.split(jax.random.key(seed), 14)
    return {
        "token_gradient": noise(seeds[0], (SEQS, SEQ_LEN, HL), 1.0, 6.0, ((0, 32), (2, 4))),
        "projection": noise(seeds[1], (D, HL), HL ** -0.5, 0.0625, ((1, 4),)),
        "clip_length": draw_clip_length(jax.random.fold_in(seeds[13], 71), 0),
        "clip_offset": draw_clip_offset(jax.random.fold_in(seeds[13], 71), 0),
        "clip_home": draw_clip_home(jax.random.fold_in(seeds[13], 71), 0),
        "block_input": noise(seeds[5], (CLIPS, FRAMES, D), 1.0, 6.0, ((0, 32),)),
        "block_output": noise(seeds[6], (CLIPS, FRAMES, D), 1.0, 6.0, ((0, 32),)),
        "norm_gain": jnp.clip(1.0 + 0.18 * jax.random.normal(seeds[7], (D,), jnp.float32), 0.1, 1.9),
        "norm_bias": noise(seeds[8], (D,), 0.5, 3.0, (), jnp.float32),
        "up_weight": noise(seeds[9], (D, FF), D ** -0.5, 0.15625, ((0, 32), (1, 4))),
        "up_bias": noise(seeds[10], (FF,), 0.5, 3.0, ((0, 4),), jnp.float32),
        "down_weight": noise(seeds[11], (FF, D), FF ** -0.5, 0.078125, ((0, 4), (1, 32))),
        "post_gain": jnp.clip(1.0 + 0.18 * jax.random.normal(seeds[12], (D,), jnp.float32), 0.1, 1.9),
    }


norm_epsilon = 1e-05

def gelu_parts(pre_act):
    normal_cdf = 0.5 * (1.0 + jax.scipy.special.erf(pre_act * 0.7071067811865476))
    normal_pdf = jnp.exp(-0.5 * pre_act * pre_act) * 0.3989422804014327
    return (pre_act * normal_cdf, normal_cdf + pre_act * normal_pdf)

def norm_stats(values):
    row_mean = lax.optimization_barrier(jnp.mean(values, axis=-1, keepdims=True))
    centred = values - row_mean
    variance = lax.optimization_barrier(jnp.mean(centred * centred, axis=-1, keepdims=True))
    inverse = lax.rsqrt(variance + norm_epsilon)
    return (centred * inverse, inverse)

def norm_backward(grad_hat, normed_hat, inverse):
    first_mean = lax.optimization_barrier(jnp.mean(grad_hat, axis=-1, keepdims=True))
    second_mean = lax.optimization_barrier(jnp.mean(grad_hat * normed_hat, axis=-1, keepdims=True))
    return inverse * (grad_hat - first_mean - normed_hat * second_mean)

def row_contract(left_rows, right_rows):
    return lax.dot_general(left_rows, right_rows, (((0,), (0,)), ((), ())), preferred_element_type=jnp.float32)

def reference(token_gradient, projection, clip_length, clip_offset, clip_home, block_input, block_output, norm_gain, norm_bias, up_weight, up_bias, down_weight, post_gain):
    positions = jnp.arange(FRAMES, dtype=jnp.int32)

    def one_clip(clip_data):
        clip_index, offset, length = clip_data
        sequence = (clip_index // CPS).astype(jnp.int32)
        picked = lax.dynamic_slice(token_gradient, (sequence, offset.astype(jnp.int32), jnp.int32(0)), (1, FRAMES, HL))[0]
        picked = jnp.where((positions < length)[:, None], picked, jnp.zeros_like(picked))
        return jnp.dot(picked, projection.T, preferred_element_type=jnp.float32).astype(jnp.bfloat16)
    projected = lax.map(one_clip, (jnp.arange(CLIPS, dtype=jnp.int32), clip_offset, clip_length))
    feature_grad = jnp.zeros((CLIPS, FRAMES, D), jnp.bfloat16).at[clip_home].set(projected)
    row_total = CLIPS * FRAMES
    feature_rows = feature_grad.reshape(row_total, D).astype(jnp.float32)
    output_hat, output_inverse = norm_stats(block_output.reshape(row_total, D).astype(jnp.float32))
    post_grad = norm_backward(feature_rows * post_gain, output_hat, output_inverse)
    post_rounded = post_grad.astype(jnp.bfloat16)
    input_hat, input_inverse = norm_stats(block_input.reshape(row_total, D).astype(jnp.float32))
    normed = (input_hat * norm_gain + norm_bias).astype(jnp.bfloat16)
    pre_act = jnp.dot(normed, up_weight, preferred_element_type=jnp.float32) + up_bias
    activation, gelu_slope = gelu_parts(pre_act)
    act_rounded = activation.astype(jnp.bfloat16)
    act_grad = jnp.dot(post_rounded, down_weight.T, preferred_element_type=jnp.float32)
    pre_grad = (act_grad * gelu_slope).astype(jnp.bfloat16)
    normed_grad = jnp.dot(pre_grad, up_weight.T, preferred_element_type=jnp.float32)
    input_rows = post_grad + norm_backward(normed_grad * norm_gain, input_hat, input_inverse)
    input_gradient = input_rows.astype(jnp.bfloat16).reshape(CLIPS, FRAMES, D)
    up_gradient = row_contract(normed, pre_grad) / CLIPS
    down_gradient = row_contract(act_rounded, post_rounded) / CLIPS
    return (input_gradient, up_gradient, down_gradient)
```

```python
import jax
import jax.numpy as jnp
from jax import lax
from jax.sharding import PartitionSpec as P

CPS = 2
SIDE = 4
CORES = 2

norm_epsilon = 1e-05


def enc_index(y, z, core):
    return ((y % SIDE) * SIDE + z % SIDE) * CORES + core % CORES


def enc_shift(dy, dz, dcore):
    return [
        (enc_index(y, z, core), enc_index(y + dy, z + dz, core + dcore))
        for y in range(SIDE)
        for z in range(SIDE)
        for core in range(CORES)
    ]


def shifted(values, axis, step):
    if axis == "llm":
        pairs = [(i, (i + step) % SIDE) for i in range(SIDE)]
        return lax.ppermute(values, "llm", pairs)
    if axis == "y":
        return lax.ppermute(values, "enc", enc_shift(step, 0, 0))
    if axis == "z":
        return lax.ppermute(values, "enc", enc_shift(0, step, 0))
    return lax.ppermute(values, "enc", enc_shift(0, 0, step))


def gelu_parts(pre_act):
    normal_cdf = 0.5 * (1.0 + jax.scipy.special.erf(pre_act * 0.7071067811865476))
    normal_pdf = jnp.exp(-0.5 * pre_act * pre_act) * 0.3989422804014327
    return (pre_act * normal_cdf, normal_cdf + pre_act * normal_pdf)


def norm_stats(values):
    row_mean = jnp.mean(values, axis=-1, keepdims=True)
    centred = values - row_mean
    variance = jnp.mean(centred * centred, axis=-1, keepdims=True)
    inverse = lax.rsqrt(variance + norm_epsilon)
    return (centred * inverse, inverse)


def norm_backward(grad_hat, normed_hat, inverse):
    first_mean = jnp.mean(grad_hat, axis=-1, keepdims=True)
    second_mean = jnp.mean(grad_hat * normed_hat, axis=-1, keepdims=True)
    return inverse * (grad_hat - first_mean - normed_hat * second_mean)


def pick(values, index, dim):
    return lax.dynamic_index_in_dim(values, index % SIDE, dim, keepdims=False)


def scatter_sum(values, axis, place, dim):
    total = pick(values, place, dim).astype(jnp.float32)
    for step in (1, 3, 2):
        block = pick(values, place + step, dim).astype(jnp.bfloat16)
        total = total + shifted(block, axis, step).astype(jnp.float32)
    return total


def gather_parts(values, axis, place, dim):
    shape = values.shape[:dim] + (SIDE,) + values.shape[dim:]
    out = jnp.zeros(shape, values.dtype)
    out = lax.dynamic_update_index_in_dim(out, values, place, dim)
    for step in (1, 3, 2):
        block = shifted(values, axis, step)
        out = lax.dynamic_update_index_in_dim(out, block, (place - step) % SIDE, dim)
    return out


def gather_weight(block, first, second, places):
    near = gather_parts(block, first, places[first], 0)
    if first == "z":
        half = gather_parts(near, second, places[second], 0)
    else:
        half = gather_parts(near, second, places[second], 1)
    other = shifted(half, "core", 1)
    core = places["core"]
    full = jnp.where(core == 0, jnp.stack([half, other], 2), jnp.stack([other, half], 2))
    return full.reshape(-1, block.shape[1])


def scatter_weight(grad, rows_here, first, second, places):
    columns = grad.shape[1]
    split = grad.reshape(SIDE, SIDE, CORES, rows_here, columns)
    core = places["core"]
    own = lax.dynamic_index_in_dim(split, core, 2, keepdims=False)
    away = lax.dynamic_index_in_dim(split, 1 - core, 2, keepdims=False)
    total = own + shifted(away.astype(jnp.bfloat16), "core", 1).astype(jnp.float32)
    dim = 0 if first == "y" else 1
    total = scatter_sum(total, first, places[first], dim)
    return scatter_sum(total, second, places[second], 0)


def row_contract(left_rows, right_rows):
    return lax.dot_general(
        left_rows, right_rows, (((0,), (0,)), ((), ())), preferred_element_type=jnp.float32
    )


def shards(
    token_gradient,
    projection,
    clip_length,
    clip_offset,
    clip_home,
    block_input,
    block_output,
    norm_gain,
    norm_bias,
    up_weight,
    up_bias,
    down_weight,
    post_gain,
):
    devices = lax.axis_size("enc")
    clips_here, frames, width = block_input.shape
    row_total = clips_here * frames
    lead = frames // SIDE
    place_x = lax.axis_index("llm")
    place_e = lax.axis_index("enc")
    places = {
        "llm": place_x,
        "y": place_e // (SIDE * CORES),
        "z": place_e // CORES % SIDE,
        "core": place_e % CORES,
    }

    up_full = gather_weight(up_weight, "z", "y", places)
    down_full = gather_weight(down_weight.T, "y", "z", places)

    clip_order = jnp.arange(clips_here, dtype=jnp.int32)
    part_rows = token_gradient.shape[1] // CPS
    local = clip_offset - clip_order % CPS * part_rows
    frame = jnp.arange(frames, dtype=jnp.int32)
    row = jnp.arange(part_rows, dtype=jnp.int32)
    hit = row[None, None, :] == local[:, None, None] + frame[None, :, None]
    live = frame[None, :, None] < clip_length[:, None, None]
    choose = (hit & live).astype(jnp.bfloat16)
    tokens = token_gradient.reshape(clips_here, part_rows, token_gradient.shape[2])
    clip_rows = jnp.einsum(
        "cfs,csw->cfw", choose, tokens, preferred_element_type=jnp.float32
    ).astype(jnp.bfloat16)
    terms = lax.dot_general(
        clip_rows.reshape(row_total, -1),
        projection,
        (((1,), (1,)), ((), ())),
        preferred_element_type=jnp.float32,
    ).reshape(clips_here, SIDE, lead, width)
    feature = scatter_sum(terms, "llm", place_x, 1).astype(jnp.bfloat16)

    target = clip_home // clips_here
    slot_place = clip_home % clips_here
    buckets = jnp.arange(devices, dtype=jnp.int32)
    routing = (buckets[:, None] == target[None, :]).astype(jnp.bfloat16)
    slot_table = (slot_place[:, None] == clip_order[None, :]).astype(jnp.bfloat16)
    marks = jnp.dot(routing, slot_table, preferred_element_type=jnp.float32)
    marks = marks.astype(jnp.bfloat16)[:, None, :]
    packed = jnp.einsum(
        "bc,cfw->bfw", routing, feature, preferred_element_type=jnp.float32
    ).astype(jnp.bfloat16)
    marks_in = lax.all_to_all(marks, "enc", split_axis=0, concat_axis=0, tiled=True)
    received = lax.all_to_all(packed, "enc", split_axis=0, concat_axis=0, tiled=True)
    placed = jnp.einsum(
        "npc,nfw->cfw", marks_in, received, preferred_element_type=jnp.float32
    ).astype(jnp.bfloat16)

    output_part = pick(
        block_output.reshape(clips_here, SIDE, lead, width), place_x, 1
    ).astype(jnp.float32)
    output_hat, output_inverse = norm_stats(output_part)
    post_part = norm_backward(
        placed.astype(jnp.float32) * post_gain, output_hat, output_inverse
    ).astype(jnp.bfloat16)
    post_rounded = gather_parts(post_part, "llm", place_x, 1).reshape(row_total, width)

    input_hat, input_inverse = norm_stats(
        block_input.reshape(row_total, width).astype(jnp.float32)
    )
    normed = (input_hat * norm_gain + norm_bias).astype(jnp.bfloat16)
    pre_act = jnp.dot(normed, up_full, preferred_element_type=jnp.float32) + up_bias
    activation, gelu_slope = gelu_parts(pre_act)
    act_rounded = activation.astype(jnp.bfloat16)
    act_grad = jnp.dot(post_rounded, down_full, preferred_element_type=jnp.float32)
    pre_grad = (act_grad * gelu_slope).astype(jnp.bfloat16)

    scale_count = clips_here * devices
    up_gradient = (
        scatter_weight(
            row_contract(normed, pre_grad), up_weight.shape[0], "z", "y", places
        )
        / scale_count
    )
    down_gradient = (
        scatter_weight(
            row_contract(post_rounded, act_rounded), down_weight.shape[1], "y", "z", places
        )
        / scale_count
    ).T

    share = width // SIDE
    normed_part = lax.dot_general(
        pre_grad, up_full, (((1,), (1,)), ((), ())), preferred_element_type=jnp.float32
    )
    grad_hat = normed_part * norm_gain
    sums = jnp.stack(
        [jnp.sum(grad_hat, -1), jnp.sum(grad_hat * input_hat, -1)], axis=-1
    )
    blocks = jnp.stack(
        [
            jnp.concatenate([normed_part[:, i * share : (i + 1) * share], sums], axis=1)
            for i in range(SIDE)
        ]
    )
    total = scatter_sum(blocks, "llm", place_x, 0)
    start = place_x * share
    gain_part = lax.dynamic_slice_in_dim(norm_gain, start, share, 0)
    hat_part = lax.dynamic_slice_in_dim(input_hat, start, share, 1)
    post_cols = lax.dynamic_slice_in_dim(post_rounded, start, share, 1).astype(jnp.float32)
    means = total[:, share:] / width
    input_rows = post_cols + input_inverse * (
        total[:, :share] * gain_part - means[:, :1] - hat_part * means[:, 1:]
    )
    input_gradient = input_rows.astype(jnp.bfloat16).reshape(clips_here, frames, share)
    return (input_gradient, up_gradient, down_gradient)


def solution(mesh):
    return jax.shard_map(
        shards,
        mesh=mesh,
        in_specs=(
            P("enc", None, "llm"),
            P(None, "llm"),
            P("enc"),
            P("enc"),
            P("enc"),
            P("enc", None, None),
            P("enc", None, None),
            P(),
            P(),
            P("enc", "llm"),
            P("llm"),
            P("llm", "enc"),
            P(),
        ),
        out_specs=(P("enc", None, "llm"), P("enc", "llm"), P("llm", "enc")),
        check_vma=False,
    )
```
